32 devices in a mesh: grp: 2 (over x), space: 16 (over z, y, core).
Axes of the slice: x: 2, y: 2, z: 4, core: 2. Of those that a mesh axis runs over, the one named last changes fastest.
Arguments:
- vectors: bfloat16 [4, 128, 6, 16, 256], P('grp', None, None, 'space'), parts along dimension 0, may hold values from -6 to 6
- gauge_links: float32 [3, 18, 4, 16, 256], P(None, None, 'grp', 'space'), parts along dimension 2, may hold values from -1.5 to 2.5, as said below
- perambulators: bfloat16 [4, 2, 2, 128, 128], P('grp'), parts along dimension 0, may hold values from -0.046875 to 0.046875
- time_pairs: int32 [16, 2], P('grp'), parts along dimension 0, may hold values from 0 to 1
- ordering: int32 [4, 128], P('grp'), parts along dimension 0, may hold values from 0 to 127, each once within a row
- op_momenta: int32 [4, 3], replicated, may hold values from -2 to 2
Outputs:
- elementals: float32 [8, 512, 128], P('grp', 'space'), parts along dimension 0
- correlators: float32 [8, 8, 2], P('grp'), parts along dimension 0
The draws below stay inside these ranges and needn't reach their ends.
There are 2 independent parts, one for each index of `grp`. The reference program is written for one: setup_inputs(seed, part) draws one part's arguments, and reference() takes and returns one part's arrays. A program takes and returns all parts, laid end to end along the dimension named above; an argument that names none is the same for every part. Nothing has to cross between parts.
Inputs may be any that keep to these rules, and one draw needn't show every extreme that they name: `gauge_links`: components ordered as row, column, then real or imaginary part of 3 x 3 complex matrices.
All inputs are finite; a program needn't handle non-finite values.
Results may differ from the reference program's by a relative error of at most 0.0051.
Values may be sent and summed in bfloat16 or wider, within the bound.
No kernel may reach another device: no remote copies, remote signals or barrier semaphores. Data moves between devices by JAX's collectives and lax.ppermute only.
A program may use at most 128 MiB of HBM per device.

```python
import math
import jax
import jax.numpy as jnp
from jax import lax

NEV = 128
NOPS = 4
SWEEPS = 2
NT = 2
LY = 16
LZ = 16
NPAIR = 8
NX = 16


def draw_gauge_links(key, part):
    full_shape = (3, 18, NT, NX, LY * LZ)
    random_part = jnp.clip(jax.random.normal(key, full_shape, jnp.float32), -5.0, 5.0) * 0.3
    component = jnp.arange(18)
    diagonal_mask = ((component == 0) | (component == 8) | (component == 16)).astype(jnp.float32)
    return random_part + diagonal_mask[None, :, None, None, None]


def set_ends(result, own_key, least, high):
    extent = result.shape
    index_at = [jax.random.randint(jax.random.fold_in(own_key, axis), (), 0, extent[axis]) for axis in range(len(extent))]
    result = result.at[tuple(index_at)].set(least)
    longest = extent.index(max(extent))
    index_at[longest] = (index_at[longest] + 1) % extent[longest]
    return result.at[tuple(index_at)].set(high)


def steps_of(rng, dims, split, low, top_value):
    loudness = 1.0
    for axis_at, shards_of in split:
        heights = jax.random.uniform(jax.random.fold_in(jax.random.fold_in(rng, 6), axis_at), (shards_of,), jnp.float32, low / len(split), top_value / len(split))
        loudness = loudness * jnp.repeat(jnp.exp(heights), dims[axis_at] // shards_of).reshape((-1,) + (1,) * (len(dims) - 1 - axis_at))
    return loudness


def normal_values(own_key, dims, width, limit, shards=(), kind=jnp.bfloat16):
    drawn = jax.random.normal(own_key, dims, jnp.float32) * width
    if len(shards) > 0:
        drawn = steps_of(own_key, dims, shards, -0.22, 0.18) * drawn
    return jnp.clip(drawn, min=-limit, max=limit).astype(kind)


def setup_inputs(seed: int = 0, part: int = 0) -> dict:
    key_of = jax.random.split(jax.random.key(seed), 7)
    part_splits = jax.random.split(jax.random.fold_in(key_of[6], part), 7)
    return {
        "vectors": normal_values(part_splits[0], (NT, NEV, 6, NX, LY * LZ), 0.7, 6.0, ((3, 16),)),
        "gauge_links": draw_gauge_links(jax.random.fold_in(jax.random.fold_in(key_of[6], part), 71), part),
        "perambulators": normal_values(part_splits[2], (NT, NT, 2, NEV, NEV), (1.0 / NEV), 0.046875),
        "time_pairs": set_ends(jax.random.randint(part_splits[3], (NPAIR, 2), 0, NT), jax.random.fold_in(part_splits[3], 1), 0, NT - 1).astype(jnp.int32),
        "ordering": jax.vmap(lambda own: jax.random.permutation(own, NEV))(jax.random.split(part_splits[4], NT)).reshape((NT, NEV)).astype(jnp.int32),
        "op_momenta": set_ends(jax.random.randint(key_of[5], (NOPS, 3), -2, 3), jax.random.fold_in(key_of[5], 1), -2, 2).astype(jnp.int32),
    }


rho_stout = 0.1
series_terms = 6


def matmul3(left_matrix, right_matrix):
    left_real, left_imag = left_matrix
    right_real, right_imag = right_matrix
    real_part = (left_real[:, :, None] * right_real[None] - left_imag[:, :, None] * right_imag[None]).sum(axis=1)
    imag_part = (left_real[:, :, None] * right_imag[None] + left_imag[:, :, None] * right_real[None]).sum(axis=1)
    return (real_part, imag_part)


def adjoint(matrix):
    return (jnp.swapaxes(matrix[0], 0, 1), -jnp.swapaxes(matrix[1], 0, 1))


def combine(first_term, second_term, weight):
    return (first_term[0] + weight * second_term[0], first_term[1] + weight * second_term[1])


def unit_step(direction, sign):
    return tuple(sign if axis_id == direction else 0 for axis_id in range(3))


def identity_like(matrix):
    diagonal_ones = jnp.eye(3, dtype=matrix[0].dtype).reshape((3, 3) + (1,) * (matrix[0].ndim - 2))
    return (jnp.broadcast_to(diagonal_ones, matrix[0].shape), jnp.zeros_like(matrix[1]))


def smear_once(fields, fetch_site):
    smeared = []
    for direction in range(3):
        centre = fetch_site(fields[direction], (0, 0, 0))
        staple_sum = None
        for other_dir in range(3):
            if other_dir == direction:
                continue
            step_ahead = unit_step(direction, 1)
            beside = unit_step(other_dir, 1)
            behind = unit_step(other_dir, -1)
            corner = tuple(step_ahead[axis_id] + behind[axis_id] for axis_id in range(3))
            upper_staple = matmul3(matmul3(fetch_site(fields[other_dir], (0, 0, 0)), fetch_site(fields[direction], beside)), adjoint(fetch_site(fields[other_dir], step_ahead)))
            lower_staple = matmul3(matmul3(adjoint(fetch_site(fields[other_dir], behind)), fetch_site(fields[direction], behind)), fetch_site(fields[other_dir], corner))
            staple_pair = combine(upper_staple, lower_staple, 1.0)
            staple_sum = staple_pair if staple_sum is None else combine(staple_sum, staple_pair, 1.0)
        omega_field = matmul3(staple_sum, adjoint(centre))
        omega_field = (rho_stout * omega_field[0], rho_stout * omega_field[1])
        flipped = adjoint(omega_field)
        half_diff = (0.5 * (omega_field[0] - flipped[0]), 0.5 * (omega_field[1] - flipped[1]))
        trace_real = (half_diff[0][0, 0] + half_diff[0][1, 1] + half_diff[0][2, 2]) / 3.0
        trace_imag = (half_diff[1][0, 0] + half_diff[1][1, 1] + half_diff[1][2, 2]) / 3.0
        unit_matrix = identity_like(centre)
        generator = (half_diff[0] - unit_matrix[0] * trace_real, half_diff[1] - unit_matrix[0] * trace_imag)
        series = unit_matrix
        for series_order in range(series_terms, 0, -1):
            series = combine(unit_matrix, matmul3(generator, series), 1.0 / series_order)
        smeared.append(matmul3(series, centre))
    return smeared


def unpack_links(stacked):
    fields = []
    for direction in range(3):
        shaped = stacked[direction].reshape((3, 3, 2) + stacked.shape[2:])
        fields.append((shaped[:, :, 0], shaped[:, :, 1]))
    return fields


def shift_sites(values, offset):
    shaped = values.reshape(values.shape[:-1] + (LY, LZ))
    shaped = jnp.roll(shaped, (-offset[0], -offset[1], -offset[2]), axis=(-3, -2, -1))
    return shaped.reshape(values.shape)


def fetch_full(matrix, offset):
    return (shift_sites(matrix[0], offset), shift_sites(matrix[1], offset))


def phase_table(momentum, x_coords, total_x):
    site_index = jnp.arange(LY * LZ, dtype=jnp.int32)
    y_coords = site_index // LZ
    z_coords = site_index % LZ
    numerator = (momentum[0] * x_coords[:, None] * (LY * LZ) + momentum[1] * y_coords[None, :] * (total_x * LZ) + momentum[2] * z_coords[None, :] * (total_x * LY)) % (total_x * LY * LZ)
    angle_value = numerator.astype(jnp.float32) * (2.0 * math.pi / (total_x * LY * LZ))
    return jnp.cos(angle_value), -jnp.sin(angle_value)


def slice_elementals(vectors, neighbours, link_real, link_imag, phase_real, phase_imag):
    count = vectors.shape[0]
    split_pairs = neighbours.reshape((count, 3, 2) + neighbours.shape[2:])
    near_real = split_pairs[:, :, 0]
    near_imag = split_pairs[:, :, 1]
    moved_real = 0.0
    moved_imag = 0.0
    for column in range(3):
        coef_real = link_real[:, column][None]
        coef_imag = link_imag[:, column][None]
        vec_real = near_real[:, column][:, None].astype(jnp.float32)
        vec_imag = near_imag[:, column][:, None].astype(jnp.float32)
        moved_real = moved_real + coef_real * vec_real - coef_imag * vec_imag
        moved_imag = moved_imag + coef_real * vec_imag + coef_imag * vec_real
    right_real = (phase_real * moved_real - phase_imag * moved_imag).astype(jnp.bfloat16)
    right_imag = (phase_real * moved_imag + phase_imag * moved_real).astype(jnp.bfloat16)
    flat_width = vectors.shape[1] * vectors.shape[2] * vectors.shape[3]
    left_rows = vectors.reshape(count, flat_width)
    stacked = jnp.concatenate([jnp.stack([right_real, right_imag], axis=2).reshape(count, flat_width), jnp.stack([right_imag, -right_real], axis=2).reshape(count, flat_width)], axis=0)
    gram_matrix = lax.dot_general(left_rows, stacked, (((1,), (1,)), ((), ())), preferred_element_type=jnp.float32)
    return gram_matrix.reshape(count, 2, count)


def pick_rows(slab_rows, order_index):
    return slab_rows[order_index]


def complex_dot(left_pair, right_pair):
    highest = lax.Precision.HIGHEST
    real_part = jnp.matmul(left_pair[0], right_pair[0], precision=highest) - jnp.matmul(left_pair[1], right_pair[1], precision=highest)
    imag_part = jnp.matmul(left_pair[0], right_pair[1], precision=highest) + jnp.matmul(left_pair[1], right_pair[0], precision=highest)
    return real_part, imag_part


def pair_trace(phi_real, phi_imag, tau_real, tau_imag, pair_row):
    source = pair_row[0]
    sink_time = pair_row[1]
    first_prod = complex_dot((phi_real[:, source], phi_imag[:, source]), (tau_real[source, sink_time], tau_imag[source, sink_time]))
    second_prod = complex_dot((phi_real[:, sink_time], phi_imag[:, sink_time]), (tau_real[sink_time, source], tau_imag[sink_time, source]))
    swap_real = jnp.swapaxes(second_prod[0], -1, -2)
    swap_imag = jnp.swapaxes(second_prod[1], -1, -2)
    trace_real = jnp.sum(first_prod[0] * swap_real - first_prod[1] * swap_imag, axis=(-2, -1))
    trace_imag = jnp.sum(first_prod[0] * swap_imag + first_prod[1] * swap_real, axis=(-2, -1))
    return jnp.stack([trace_real, trace_imag], axis=-1)


def reference(vectors, gauge_links, perambulators, time_pairs, ordering, op_momenta):
    fields = unpack_links(gauge_links)
    for sweep_index in range(SWEEPS):
        fields = smear_once(fields, fetch_full)
    ordered = jax.vmap(pick_rows)(vectors, ordering)
    total_x = gauge_links.shape[3]
    x_coords = jnp.arange(total_x, dtype=jnp.int32)
    scale_factor = (3.0 * total_x * LY * LZ) ** -0.5
    results = []
    for operator in range(NOPS):
        direction = operator % 3
        neighbours = shift_sites(ordered, unit_step(direction, 1))
        phase_real, phase_imag = phase_table(op_momenta[operator], x_coords, total_x)
        link_real = jnp.moveaxis(fields[direction][0], 2, 0)
        link_imag = jnp.moveaxis(fields[direction][1], 2, 0)

        def one_slice(slice_items, phase_real=phase_real, phase_imag=phase_imag):
            return slice_elementals(slice_items[0], slice_items[1], slice_items[2], slice_items[3], phase_real, phase_imag)

        per_slice = lax.map(one_slice, (ordered, neighbours, link_real, link_imag))
        results.append(per_slice.reshape(-1, per_slice.shape[-1]) * scale_factor)
    elementals = jnp.stack(results)
    phi_full = elementals.reshape(NOPS, NT, NEV, 2, NEV)
    phi_real = phi_full[:, :, :, 0]
    phi_imag = phi_full[:, :, :, 1]
    tau_real = perambulators[:, :, 0].astype(jnp.float32)
    tau_imag = perambulators[:, :, 1].astype(jnp.float32)
    traces = lax.map(lambda pair_row: pair_trace(phi_real, phi_imag, tau_real, tau_imag, pair_row), time_pairs)
    correlators = jnp.transpose(traces, (1, 0, 2))
    return (elementals, correlators)
```

```python
import math

import jax
import jax.numpy as jnp
from jax import lax
from jax.experimental import pallas as pl
from jax.experimental.pallas import tpu as pltpu
from jax.sharding import PartitionSpec as P

LY = 16
LZ = 16
RHO = 0.1


F32 = jnp.float32
BF16 = jnp.bfloat16


def vmem():
    return pl.BlockSpec(memory_space=pltpu.VMEM)


def smem():
    return pl.BlockSpec(memory_space=pltpu.SMEM)


def call(kernel, outs, ins, scalars=0, scratch=(), name=None, flops=1000000):
    return pl.pallas_call(
        kernel,
        out_shape=[jax.ShapeDtypeStruct(s, d) for s, d in outs],
        in_specs=[smem()] * scalars + [vmem()] * (len(ins) - scalars),
        out_specs=[vmem()] * len(outs),
        scratch_shapes=list(scratch),
        name=name,
        cost_estimate=pl.CostEstimate(flops=flops, bytes_accessed=1000000, transcendentals=0),
    )(*ins)


def shifted(value, by):
    size = lax.axis_size("space")
    return lax.ppermute(value, "space", [(i, (i + by) % size) for i in range(size)])


def swapped(value, bit):
    size = lax.axis_size("space")
    return lax.ppermute(value, "space", [(i, i ^ bit) for i in range(size)])


def cmul(x, y):
    return (x[0] * y[0] - x[1] * y[1], x[0] * y[1] + x[1] * y[0])


def cadd(x, y):
    return (x[0] + y[0], x[1] + y[1])


def conj_mul(x, y):
    return (x[0] * y[0] + x[1] * y[1], x[0] * y[1] - x[1] * y[0])


def mul_conj(x, y):
    return (x[0] * y[0] + x[1] * y[1], x[1] * y[0] - x[0] * y[1])


def total(terms):
    out = terms[0]
    for t in terms[1:]:
        out = cadd(out, t)
    return out


R3 = range(3)


def mm(x, y):
    return [[total([cmul(x[a][c], y[c][b]) for c in R3]) for b in R3] for a in R3]


def mm_h(x, y):
    return [[total([mul_conj(x[a][c], y[b][c]) for c in R3]) for b in R3] for a in R3]


def h_mm(x, y):
    return [[total([conj_mul(x[c][a], y[c][b]) for c in R3]) for b in R3] for a in R3]


OFF = ((0, 1), (0, 2), (1, 2))


def anti(entry, imag):
    out = [imag(a, a) for a in R3]
    for a, b in OFF:
        up, low = entry(a, b), entry(b, a)
        out += [up[0] - low[0], up[1] + low[1]]
    return out


def anti_mm(x, y):
    def imag(a, b):
        terms = [x[a][c][0] * y[c][b][1] + x[a][c][1] * y[c][b][0] for c in R3]
        return terms[0] + terms[1] + terms[2]

    return anti(lambda a, b: total([cmul(x[a][c], y[c][b]) for c in R3]), imag)


def anti_mm_h(x, y):
    def imag(a, b):
        terms = [x[a][c][1] * y[b][c][0] - x[a][c][0] * y[b][c][1] for c in R3]
        return terms[0] + terms[1] + terms[2]

    return anti(lambda a, b: total([mul_conj(x[a][c], y[b][c]) for c in R3]), imag)


def exp_series(w):
    mean = (w[0] + w[1] + w[2]) * (RHO / 3.0)
    h = [w[a] * RHO - mean for a in R3]
    z = {}
    for at, (a, b) in enumerate(OFF):
        z[a, b] = (w[3 + 2 * at] * (0.5 * RHO), w[4 + 2 * at] * (0.5 * RHO))
    size = {ab: v[0] * v[0] + v[1] * v[1] for ab, v in z.items()}
    s_diag = [
        -(h[0] * h[0] + size[0, 1] + size[0, 2]),
        -(h[1] * h[1] + size[0, 1] + size[1, 2]),
        -(h[2] * h[2] + size[0, 2] + size[1, 2]),
    ]

    def turned(v, by):
        return (-by * v[1], by * v[0])

    neg = lambda v: (-v[0], -v[1])
    s = {
        (0, 1): cadd(turned(z[0, 1], h[0] + h[1]), neg(mul_conj(z[0, 2], z[1, 2]))),
        (0, 2): cadd(turned(z[0, 2], h[0] + h[2]), cmul(z[0, 1], z[1, 2])),
        (1, 2): cadd(turned(z[1, 2], h[1] + h[2]), neg(conj_mul(z[0, 1], z[0, 2]))),
    }
    p = 0.5 * (s_diag[0] + s_diag[1] + s_diag[2])
    ha, hb, hc = [(z[ab][1], -z[ab][0]) for ab in OFF]
    triple = cmul(ha, hc)
    det = (
        h[0] * (h[1] * h[2] - size[1, 2])
        - h[1] * size[0, 2]
        - h[2] * size[0, 1]
        + 2.0 * (triple[0] * hb[0] + triple[1] * hb[1])
    )
    k = -det
    f0 = (1.0 - (k * (1.0 / 720.0)) * k, k * (1.0 / 6.0 + p * (1.0 / 120.0)))
    f1 = (1.0 + p * (1.0 / 6.0) + (p * (1.0 / 120.0)) * p, k * (1.0 / 24.0 + p * (1.0 / 360.0)))
    f2 = (0.5 + p * (1.0 / 24.0) + (p * (1.0 / 720.0)) * p, k * (1.0 / 120.0))
    out = [[None] * 3 for _ in R3]
    for a in R3:
        out[a][a] = (
            f0[0] - f1[1] * h[a] + f2[0] * s_diag[a],
            f0[1] + f1[0] * h[a] + f2[1] * s_diag[a],
        )
    for a, b in OFF:
        (zr, zi), (sr, si) = z[a, b], s[a, b]
        rr, ri, ir, ii = f1[0] * zr, f1[0] * zi, f1[1] * zr, f1[1] * zi
        tr, ti, ur, ui = f2[0] * sr, f2[0] * si, f2[1] * sr, f2[1] * si
        out[a][b] = (rr - ii + tr - ui, ri + ir + ti + ur)
        out[b][a] = (tr + ui - rr - ii, ri - ir + ur - ti)
    return out


def smear_kernel(below2, below, own, above, above2, out, links, moved):
    rows = own.shape[1]
    planes = (below2, below, own, above, above2)
    for at, plane in enumerate(planes):
        links[0, :, rows * at : rows * (at + 1), :] = plane[...]
    tile = 2 * rows
    lane = lax.broadcasted_iota(jnp.int32, (tile, 128), 1)
    row = lax.broadcasted_iota(jnp.int32, (tile, 128), 0)
    even = (row & 1) == 0
    z_at = lane & (LZ - 1)

    def flip(x):
        return jnp.where(even, pltpu.roll(x, tile - 1, 0), pltpu.roll(x, 1, 0))

    def ahead_y(x):
        x = pltpu.roll(x, 128 - LZ, 1)
        return jnp.where(lane < 128 - LZ, x, flip(x))

    def behind_y(x):
        x = pltpu.roll(x, LZ, 1)
        return jnp.where(lane >= LZ, x, flip(x))

    def ahead_z(x):
        return jnp.where(z_at < LZ - 1, pltpu.roll(x, 127, 1), pltpu.roll(x, LZ - 1, 1))

    def behind_z(x):
        return jnp.where(z_at > 0, pltpu.roll(x, 1, 1), pltpu.roll(x, 128 - LZ + 1, 1))

    moved[...] = jnp.zeros_like(moved)

    def step(j, carry):
        source = jnp.where(j == 2, 1, 0)
        base = jnp.where(j == 2, rows, tile * j)
        target = jnp.where(j == 2, 2, 1)
        write = jnp.where(j == 2, 0, tile * j)
        base = pl.multiple_of(base, rows)
        write = pl.multiple_of(write, rows)

        def raw(c, off=0):
            return links[source, c, pl.ds(base + off, tile), :]

        def matrix(m, move=None, off=0):
            move = move or (lambda v: v)
            at = lambda a, b, r: move(raw(18 * m + 2 * (3 * a + b) + r, off))
            return [[(at(a, b, 0), at(a, b, 1)) for b in R3] for a in R3]

        def ahead(m, n):
            if n == 0:
                return matrix(m, None, rows)
            return matrix(m, ahead_y if n == 1 else ahead_z)

        def behind(values, n, slot):
            if n == 1:
                return [behind_y(v) for v in values]
            if n == 2:
                return [behind_z(v) for v in values]
            back = []
            for c, v in enumerate(values):
                moved[source, 9 * slot + c, pl.ds(base + rows, tile), :] = v
                back.append(moved[source, 9 * slot + c, pl.ds(base, tile), :])
            return back

        w = [None, None, None]

        def give(m, values, sign):
            if w[m] is None:
                assert sign > 0
                w[m] = values
            else:
                w[m] = [a + b if sign > 0 else a - b for a, b in zip(w[m], values)]

        for m, n in ((0, 1), (2, 0), (1, 2)):
            um, un = matrix(m), matrix(n)
            y = mm_h(ahead(n, m), ahead(m, n))
            x = h_mm(un, um)
            plaq = anti_mm_h(mm_h(un, y), um)
            give(m, plaq, 1)
            q_m = anti_mm(x, y)
            q_n = anti_mm(y, x)
            slot = 0 if 1 in (m, n) else 1
            give(m, behind(q_m, n, slot), 1)
            if w[n] is None:
                w[n] = [-a for a in plaq]
            else:
                give(n, plaq, -1)
            give(n, behind(q_n, m, slot), -1)
        for m in R3:
            new = mm(exp_series(w[m]), matrix(m))
            for a in R3:
                for b in R3:
                    for r in range(2):
                        c = 18 * m + 2 * (3 * a + b) + r
                        links[target, c, pl.ds(write, tile), :] = new[a][b][r]
        return carry

    lax.fori_loop(0, 3, step, 0)
    out[...] = links[2, :, rows:tile, :]


def order_kernel(ordering, vectors, out):
    nt, comps, count, sites = vectors.shape
    row = lax.broadcasted_iota(jnp.int32, (count, count), 0)
    for t in range(nt):
        hot = jnp.where(row == ordering[t : t + 1, :], 1.0, 0.0).T.astype(BF16)
        for c in range(comps):
            a, r = c // 2, c % 2
            picked = jnp.dot(hot, vectors[t, c], preferred_element_type=F32)
            out[t, r * count : (r + 1) * count, a * sites : (a + 1) * sites] = picked.astype(BF16)


def move_kernel(total_x, pos, momenta, ordered, out_y, out_z, phase):
    nt, rows, width = ordered.shape
    sites = width // 3
    src = lax.broadcasted_iota(jnp.int32, (sites, sites), 0)
    dst = lax.broadcasted_iota(jnp.int32, (sites, sites), 1)
    to_y = (dst + LZ) & (sites - 1)
    to_z = jnp.where((dst & (LZ - 1)) < LZ - 1, dst + 1, dst - (LZ - 1))
    for out, to in ((out_y, to_y), (out_z, to_z)):
        hot = jnp.where(src == to, 1.0, 0.0).astype(BF16)
        for t in range(nt):
            for a in range(3):
                at = slice(a * sites, (a + 1) * sites)
                out[t, :, at] = jnp.dot(
                    ordered[t, :, at], hot, preferred_element_type=F32
                ).astype(BF16)
    nops = momenta.shape[0]
    shape = (2 * nops, 128)
    row = lax.broadcasted_iota(jnp.int32, shape, 0)
    site = (row & 1) * 128 + lax.broadcasted_iota(jnp.int32, shape, 1)
    y_at, z_at = site // LZ, site & (LZ - 1)
    period = total_x * LY * LZ
    number = jnp.zeros(shape, jnp.int32)
    for k in range(nops):
        here = (
            momenta[k, 0] * pos[0] * (LY * LZ)
            + momenta[k, 1] * y_at * (total_x * LZ)
            + momenta[k, 2] * z_at * (total_x * LY)
        )
        number = jnp.where((row >> 1) == k, here, number)
    number = number & (period - 1)
    quarter = period // 4
    turn = (number + quarter // 2) // quarter
    angle = (number - turn * quarter).astype(F32) * (2.0 * math.pi / period)
    sq = angle * angle
    sin = 1.0 / 362880.0
    for d in (-5040.0, 120.0, -6.0, 1.0):
        sin = sin * sq + 1.0 / d
    sin = sin * angle
    cos = -1.0 / 3628800.0
    for d in (40320.0, -720.0, 24.0, -2.0, 1.0):
        cos = cos * sq + 1.0 / d
    turn = turn & 3
    odd = (turn & 1) == 1
    big, small = jnp.where(odd, sin, cos), jnp.where(odd, cos, sin)
    phase[0] = jnp.where((turn == 1) | (turn == 2), -big, big)
    phase[1] = -jnp.where(turn >= 2, -small, small)


def elemental_kernel(scale, which, pos, links, phase, ordered, near_x, near_y, near_z, out, right):
    nt, rows, width = ordered.shape
    count, sites = rows // 2, width // 3
    nops = phase.shape[1] // 2
    t = (pos[0] + which) & (nt - 1)
    sub = 16
    for k in range(nops):
        m = k % 3
        near = (near_x, near_y, near_z)[m]
        buf = k % 2
        for h in range(2):
            row = 2 * t + h
            pr = phase[0, 2 * k + h : 2 * k + h + 1, :]
            pi = phase[1, 2 * k + h : 2 * k + h + 1, :]
            coef = []
            for e in range(9):
                cr = links[18 * m + 2 * e, pl.ds(row, 1), :]
                ci = links[18 * m + 2 * e + 1, pl.ds(row, 1), :]
                coef.append(
                    [
                        jnp.broadcast_to(v, (sub, 128))
                        for v in (pr * cr - pi * ci, pr * ci + pi * cr)
                    ]
                )

            def block(i, carry, near=near, coef=coef, h=h, buf=buf):
                i0 = pl.multiple_of(i * sub, sub)
                v = []
                for b in range(3):
                    lo = b * sites + h * 128
                    v.append(
                        [
                            near[t, pl.ds(i0 + r * count, sub), lo : lo + 128].astype(F32)
                            for r in range(2)
                        ]
                    )
                for a in range(3):
                    got = total([cmul(coef[3 * a + b], v[b]) for b in range(3)])
                    lo = a * sites + h * 128
                    for r in range(2):
                        right[buf, pl.ds(i0 + r * count, sub), lo : lo + 128] = got[r].astype(BF16)
                return carry

            lax.fori_loop(0, count // sub, block, 0, unroll=True)
        gram = lax.dot_general(
            ordered[t], right[buf], (((1,), (1,)), ((), ())), preferred_element_type=F32
        )
        out[k, 0] = (gram[:count, :count] + gram[count:, count:]) * scale
        out[k, 1] = (gram[:count, count:] - gram[count:, :count]) * scale


def split_kernel(bit, pos, mine, other, send, keep):
    half = keep.shape[0]
    up = (pos[0] >> bit) & 1
    at_send, at_keep = (1 - up) * half, up * half
    for j in range(half):
        send[j] = (mine[at_send + j] + other[at_send + j].astype(F32)).astype(send.dtype)
        keep[j] = mine[at_keep + j] + other[at_keep + j].astype(F32)


def add_kernel(mine, other, out):
    out[...] = (mine[...].astype(F32) + other[...].astype(F32)).astype(out.dtype)


def block_rows(ref, d, per):
    return ref[:, d % per]


def trace_kernel(pos, mine, other, mine_b, other_b, tau, keep, send):
    nt, count = tau.shape[0], tau.shape[-1]
    parity = pos[0] & (nt - 1)
    per, ib = mine_b.shape[1], mine_b.shape[2]
    for out, flips in ((send, (2, 6)), (keep, (0, 4))):
        for at, f in enumerate(flips):
            d = pos[0] ^ f
            a, b = mine_b[:, d % per], other_b[:, d % per]
            use = (d // per) == parity
            picked = jnp.where(use, a, b)
            for r in range(2):
                lo = (2 * at + r) * ib
                out[lo : lo + ib, :] = picked[r]
    phi = []
    for t in range(nt):
        own, oth = mine[...], other[...]
        x = jnp.where(parity == t, own, oth).reshape(2 * count, count)
        hi = x.astype(BF16)
        lo = (x - hi.astype(F32)).astype(BF16)
        phi.append(jnp.concatenate([hi, lo], axis=0))
    prod = {}
    for t in range(nt):
        for u in range(nt):
            right = jnp.concatenate([tau[t, u, 0], tau[t, u, 1]], axis=1)
            got = jnp.dot(phi[t], right, preferred_element_type=F32)
            got = got[: 2 * count] + got[2 * count :]
            prod[t, u] = (
                got[:count, :count] - got[count:, count:],
                got[:count, count:] + got[count:, :count],
            )
    rows = []
    for t in range(nt):
        for u in range(t, nt):
            xr, xi = prod[t, u]
            yr, yi = prod[u, t][0].T, prod[u, t][1].T
            rows.append(jnp.sum(xr * yr - xi * yi, axis=0, keepdims=True))
            rows.append(jnp.sum(xr * yi + xi * yr, axis=0, keepdims=True))
    base = 4 * ib
    for out in (send, keep):
        for at, v in enumerate(rows):
            out[base + at : base + at + 1, :] = v
        out[base + len(rows) :, :] = jnp.zeros_like(out[base + len(rows) :, :])


def middle_kernel(ib, pos, mine, other, keep, send):
    up = ((pos[0] >> 1) & 1) == 1
    a, b = mine[...], other[...]
    pair = (jnp.where(up, b, a), jnp.where(up, a, b))
    tail = a.shape[0] - 4 * ib
    size = 2 * ib + tail
    for at, v in enumerate(pair):
        lo = at * size
        keep[lo : lo + 2 * ib, :] = v[: 2 * ib]
        send[lo : lo + 2 * ib, :] = v[2 * ib : 4 * ib]
        keep[lo + 2 * ib : lo + size, :] = v[4 * ib :]
        send[lo + 2 * ib : lo + size, :] = v[4 * ib :]


def final_kernel(ib, nt, pos, mine, other, pairs, out, corr):
    up = ((pos[0] >> 2) & 1) == 1
    a, b = mine[...], other[...]
    pair = (jnp.where(up, b, a), jnp.where(up, a, b))
    size = a.shape[0] // 2
    first, second = pairs[0:1, :], pairs[1:2, :]
    low, high = jnp.minimum(first, second), jnp.maximum(first, second)
    index = low * nt - (low * (low - 1)) // 2 + (high - low)
    combos = nt * (nt + 1) // 2
    for k in range(4):
        v = pair[k & 1][(k >> 1) * size : (k >> 1) * size + size]
        for r in range(2):
            out[k, pl.ds(r, ib, stride=2), :] = v[r * ib : (r + 1) * ib]
        sums = jnp.sum(v[2 * ib :], axis=1, keepdims=True)
        for r in range(2):
            line = jnp.zeros(index.shape, F32)
            for j in range(combos):
                value = jnp.broadcast_to(sums[2 * j + r : 2 * j + r + 1, :], index.shape)
                line = jnp.where(index == j, value, line)
            corr[k, r : r + 1, :] = line


def on_device(vectors, gauge_links, perambulators, time_pairs, ordering, op_momenta):
    devices = lax.axis_size("space")
    pos = lax.axis_index("space").astype(jnp.int32).reshape(1)
    nt, count, comps, planes, sites = vectors.shape
    nops = op_momenta.shape[0]
    total_x = planes * devices
    assert planes == 1 and nt == 2 and nops == 4 and devices >= 8
    assert devices & (devices - 1) == 0 and sites == LY * LZ == 256
    scale = (3.0 * total_x * LY * LZ) ** (-0.5)

    own = gauge_links.reshape(54, nt * 2, 128)
    below, above = shifted(own, 1), shifted(own, -1)
    below2, above2 = shifted(own, 2), shifted(own, -2)

    natural = jnp.transpose(vectors, (0, 2, 3, 1, 4)).reshape(nt, comps, count, sites)
    wide = (nt, 2 * count, 3 * sites)
    (ordered,) = call(order_kernel, [(wide, BF16)], [ordering, natural], name="order")
    near_x = shifted(ordered, -1)
    near_y, near_z, phase = call(
        lambda *refs: move_kernel(total_x, *refs),
        [(wide, BF16), (wide, BF16), ((2, 2 * nops, 128), F32)],
        [pos, op_momenta, ordered],
        scalars=2,
        name="move",
    )
    rows = nt * 2
    (smeared,) = call(
        smear_kernel,
        [((54, rows, 128), F32)],
        [below2, below, own, above, above2],
        scratch=[
            pltpu.VMEM((3, 54, 6 * rows, 128), F32),
            pltpu.VMEM((2, 18, 6 * rows, 128), F32),
        ],
        name="smear",
    )

    def grams(which):
        (out,) = call(
            lambda *refs: elemental_kernel(scale, which, *refs),
            [((nops, 2, count, count), F32)],
            [pos, smeared, phase, ordered, near_x, near_y, near_z],
            scalars=1,
            scratch=[pltpu.VMEM((2, 2 * count, 3 * sites), BF16)],
            name="elementals",
        )
        return out

    away = swapped(grams(1), 1)
    held = grams(0)
    flat = (2, count, count)
    send, keep = call(
        lambda *refs: split_kernel(1, *refs),
        [((2,) + flat, BF16), ((2,) + flat, F32)],
        [pos, held, away],
        scalars=1,
        name="split",
    )
    send, keep = call(
        lambda *refs: split_kernel(2, *refs),
        [((1,) + flat, BF16), ((1,) + flat, F32)],
        [pos, keep, swapped(send, 2)],
        scalars=1,
        name="split",
    )
    bit = 8
    other = swapped(send, 4)
    while bit <= devices:
        (keep,) = call(
            add_kernel, [((1,) + flat, BF16 if bit < devices else F32)], [keep, other], name="add"
        )
        other = swapped(keep, bit if bit < devices else 1)
        bit *= 2
    mine, other = keep.reshape(flat), other.reshape(flat)
    ib = nt * count // devices
    per = devices // nt
    size = 4 * ib + 8
    keep, send = call(
        trace_kernel,
        [((size, 128), F32)] * 2,
        [
            pos,
            mine,
            other,
            mine.reshape(2, per, ib, count),
            other.reshape(2, per, ib, count),
            perambulators,
        ],
        scalars=1,
        name="traces",
    )
    keep, send = call(
        lambda *refs: middle_kernel(ib, *refs),
        [((2 * (2 * ib + 8), 128), F32)] * 2,
        [pos, keep, swapped(send, 2)],
        scalars=1,
        name="middle",
    )
    out, corr = call(
        lambda *refs: final_kernel(ib, nt, *refs),
        [((nops, 2 * ib, count), F32), ((nops, 2, time_pairs.shape[0]), F32)],
        [pos, keep, swapped(send, 4), time_pairs.T],
        scalars=1,
        name="final",
    )
    return out, jnp.transpose(corr, (0, 2, 1))


def solution(mesh):
    return jax.shard_map(
        on_device,
        mesh=mesh,
        in_specs=(
            P("grp", None, None, "space", None),
            P(None, None, "grp", "space", None),
            P("grp", None, None, None, None),
            P("grp", None),
            P("grp", None),
            P(),
        ),
        out_specs=(P("grp", "space", None), P("grp", None, None)),
        check_vma=False,
    )
```

```python
import math

import jax
import jax.numpy as jnp
from jax import lax
from jax.experimental import pallas as pl
from jax.experimental.pallas import tpu as pltpu
from jax.sharding import PartitionSpec as P


LY = 16
LZ = 16
RHO = 0.1


F32 = jnp.float32
BF16 = jnp.bfloat16


def vmem():
    return pl.BlockSpec(memory_space=pltpu.VMEM)


def smem():
    return pl.BlockSpec(memory_space=pltpu.SMEM)


def call(kernel, outs, ins, scalars=0, scratch=(), loose=0, flops=1000000, limit=16 << 20):
    run = pl.pallas_call(
        kernel,
        out_shape=[jax.ShapeDtypeStruct(s, d) for s, d in outs],
        in_specs=[smem()] * scalars
        + [vmem()] * (len(ins) - scalars - loose)
        + [pl.BlockSpec(memory_space=pltpu.HBM)] * loose,
        out_specs=[vmem()] * len(outs),
        scratch_shapes=list(scratch),
        compiler_params=pltpu.CompilerParams(vmem_limit_bytes=limit),
        cost_estimate=pl.CostEstimate(flops=flops, bytes_accessed=1000000, transcendentals=0),
    )
    first = len(ins) - loose
    ins = ins[:first] + [pltpu.with_memory_space_constraint(x, pltpu.HBM) for x in ins[first:]]
    return run(*ins)


def shifted(value, by):
    size = lax.axis_size("space")
    return lax.ppermute(value, "space", [(i, (i + by) % size) for i in range(size)])


def swapped(value, bit):
    size = lax.axis_size("space")
    return lax.ppermute(value, "space", [(i, i ^ bit) for i in range(size)])


def cmul(x, y):
    return (x[0] * y[0] - x[1] * y[1], x[0] * y[1] + x[1] * y[0])


def cadd(x, y):
    return (x[0] + y[0], x[1] + y[1])


def conj_mul(x, y):
    return (x[0] * y[0] + x[1] * y[1], x[0] * y[1] - x[1] * y[0])


def mul_conj(x, y):
    return (x[0] * y[0] + x[1] * y[1], x[1] * y[0] - x[0] * y[1])


def total(terms):
    out = terms[0]
    for t in terms[1:]:
        out = cadd(out, t)
    return out


R3 = range(3)


def mm(x, y):
    return [[total([cmul(x[a][c], y[c][b]) for c in R3]) for b in R3] for a in R3]


def mm_h(x, y):
    return [[total([mul_conj(x[a][c], y[b][c]) for c in R3]) for b in R3] for a in R3]


def h_mm(x, y):
    return [[total([conj_mul(x[c][a], y[c][b]) for c in R3]) for b in R3] for a in R3]


OFF = ((0, 1), (0, 2), (1, 2))


def anti(entry, imag):
    out = [imag(a, a) for a in R3]
    for a, b in OFF:
        up, low = entry(a, b), entry(b, a)
        out += [up[0] - low[0], up[1] + low[1]]
    return out


def anti_mm(x, y):
    def imag(a, b):
        terms = [x[a][c][0] * y[c][b][1] + x[a][c][1] * y[c][b][0] for c in R3]
        return terms[0] + terms[1] + terms[2]

    return anti(lambda a, b: total([cmul(x[a][c], y[c][b]) for c in R3]), imag)


def anti_mm_h(x, y):
    def imag(a, b):
        terms = [x[a][c][1] * y[b][c][0] - x[a][c][0] * y[b][c][1] for c in R3]
        return terms[0] + terms[1] + terms[2]

    return anti(lambda a, b: total([mul_conj(x[a][c], y[b][c]) for c in R3]), imag)


def exp_series(w):
    mean = (w[0] + w[1] + w[2]) * (RHO / 3.0)
    h = [w[a] * RHO - mean for a in R3]
    z = {}
    for at, (a, b) in enumerate(OFF):
        z[a, b] = (w[3 + 2 * at] * (0.5 * RHO), w[4 + 2 * at] * (0.5 * RHO))
    size = {ab: v[0] * v[0] + v[1] * v[1] for ab, v in z.items()}
    s_diag = [
        -(h[0] * h[0] + size[0, 1] + size[0, 2]),
        -(h[1] * h[1] + size[0, 1] + size[1, 2]),
        -(h[2] * h[2] + size[0, 2] + size[1, 2]),
    ]

    def turned(v, by):
        return (-by * v[1], by * v[0])

    neg = lambda v: (-v[0], -v[1])
    s = {
        (0, 1): cadd(turned(z[0, 1], h[0] + h[1]), neg(mul_conj(z[0, 2], z[1, 2]))),
        (0, 2): cadd(turned(z[0, 2], h[0] + h[2]), cmul(z[0, 1], z[1, 2])),
        (1, 2): cadd(turned(z[1, 2], h[1] + h[2]), neg(conj_mul(z[0, 1], z[0, 2]))),
    }
    p = 0.5 * (s_diag[0] + s_diag[1] + s_diag[2])
    ha, hb, hc = [(z[ab][1], -z[ab][0]) for ab in OFF]
    triple = cmul(ha, hc)
    det = (
        h[0] * (h[1] * h[2] - size[1, 2])
        - h[1] * size[0, 2]
        - h[2] * size[0, 1]
        + 2.0 * (triple[0] * hb[0] + triple[1] * hb[1])
    )
    k = -det
    f0 = (1.0 - (k * (1.0 / 720.0)) * k, k * (1.0 / 6.0 + p * (1.0 / 120.0)))
    f1 = (1.0 + p * (1.0 / 6.0) + (p * (1.0 / 120.0)) * p, k * (1.0 / 24.0 + p * (1.0 / 360.0)))
    f2 = (0.5 + p * (1.0 / 24.0) + (p * (1.0 / 720.0)) * p, k * (1.0 / 120.0))
    out = [[None] * 3 for _ in R3]
    for a in R3:
        out[a][a] = (
            f0[0] - f1[1] * h[a] + f2[0] * s_diag[a],
            f0[1] + f1[0] * h[a] + f2[1] * s_diag[a],
        )
    for a, b in OFF:
        (zr, zi), (sr, si) = z[a, b], s[a, b]
        rr, ri, ir, ii = f1[0] * zr, f1[0] * zi, f1[1] * zr, f1[1] * zi
        tr, ti, ur, ui = f2[0] * sr, f2[0] * si, f2[1] * sr, f2[1] * si
        out[a][b] = (rr - ii + tr - ui, ri + ir + ti + ur)
        out[b][a] = (tr + ui - rr - ii, ri - ir + ur - ti)
    return out


def pack_kernel(pos, links, links_in, chip, edge_up, edge_down):
    second = (pos[0] & 1) == 1
    half = links.shape[1]
    a, b = links[...], links_in[...]
    planes = (jnp.where(second, b, a), jnp.where(second, a, b))
    high = [v.astype(BF16) for v in planes]
    low = [(v - h.astype(F32)).astype(BF16) for v, h in zip(planes, high)]
    for at in range(2):
        chip[:, half * at : half * (at + 1), :] = planes[at]
    for out, parts in ((edge_up, high + [low[1]]), (edge_down, high + [low[0]])):
        for at, v in enumerate(parts):
            out[:, half * at : half * (at + 1), :] = v


def smear_kernel(below, own, above, out, links, moved):
    rows = own.shape[1] // 2
    low, high = below[...].astype(F32), above[...].astype(F32)
    parts = (
        low[:, :rows],
        low[:, rows : 2 * rows] + low[:, 2 * rows :],
        own[:, :rows],
        own[:, rows:],
        high[:, :rows] + high[:, 2 * rows :],
        high[:, rows : 2 * rows],
    )
    for at, part in enumerate(parts):
        links[0, :, rows * at : rows * (at + 1), :] = part
    tile = 4 * rows
    lane = lax.broadcasted_iota(jnp.int32, (tile, 128), 1)
    row = lax.broadcasted_iota(jnp.int32, (tile, 128), 0)
    even = (row & 1) == 0
    z_at = lane & (LZ - 1)

    def flip(x):
        return jnp.where(even, pltpu.roll(x, tile - 1, 0), pltpu.roll(x, 1, 0))

    def ahead_y(x):
        x = pltpu.roll(x, 128 - LZ, 1)
        return jnp.where(lane < 128 - LZ, x, flip(x))

    def behind_y(x):
        x = pltpu.roll(x, LZ, 1)
        return jnp.where(lane >= LZ, x, flip(x))

    def ahead_z(x):
        return jnp.where(z_at < LZ - 1, pltpu.roll(x, 127, 1), pltpu.roll(x, LZ - 1, 1))

    def behind_z(x):
        return jnp.where(z_at > 0, pltpu.roll(x, 1, 1), pltpu.roll(x, 128 - LZ + 1, 1))

    moved[...] = jnp.zeros_like(moved)

    def step(j, carry):
        source = jnp.where(j == 2, 1, 0)
        base = jnp.where(j == 2, rows, tile * j)
        target = jnp.where(j == 2, 2, 1)
        write = jnp.where(j == 2, 0, tile * j)
        base = pl.multiple_of(base, rows)
        write = pl.multiple_of(write, rows)

        def raw(c, off=0):
            return links[source, c, pl.ds(base + off, tile), :]

        def matrix(m, move=None, off=0):
            move = move or (lambda v: v)
            at = lambda a, b, r: move(raw(18 * m + 2 * (3 * a + b) + r, off))
            return [[(at(a, b, 0), at(a, b, 1)) for b in R3] for a in R3]

        def ahead(m, n):
            if n == 0:
                return matrix(m, None, rows)
            return matrix(m, ahead_y if n == 1 else ahead_z)

        def behind(values, n, slot):
            if n == 1:
                return [behind_y(v) for v in values]
            if n == 2:
                return [behind_z(v) for v in values]
            back = []
            for c, v in enumerate(values):
                moved[source, 9 * slot + c, pl.ds(base + rows, tile), :] = v
                back.append(moved[source, 9 * slot + c, pl.ds(base, tile), :])
            return back

        w = [None, None, None]

        def give(m, values, sign):
            if w[m] is None:
                assert sign > 0
                w[m] = values
            else:
                w[m] = [a + b if sign > 0 else a - b for a, b in zip(w[m], values)]

        for m, n in ((0, 1), (2, 0), (1, 2)):
            um, un = matrix(m), matrix(n)
            y = mm_h(ahead(n, m), ahead(m, n))
            x = h_mm(un, um)
            plaq = anti_mm_h(mm_h(un, y), um)
            give(m, plaq, 1)
            q_m = anti_mm(x, y)
            q_n = anti_mm(y, x)
            slot = 0 if 1 in (m, n) else 1
            give(m, behind(q_m, n, slot), 1)
            if w[n] is None:
                w[n] = [-a for a in plaq]
            else:
                give(n, plaq, -1)
            give(n, behind(q_n, m, slot), -1)
        for m in R3:
            new = mm(exp_series(w[m]), matrix(m))
            for a in R3:
                for b in R3:
                    for r in range(2):
                        c = 18 * m + 2 * (3 * a + b) + r
                        links[target, c, pl.ds(write, tile), :] = new[a][b][r]
        return carry

    lax.fori_loop(0, 3, step, 0)
    out[...] = links[2, :, rows : 3 * rows, :]


def split_links_kernel(pos, links, keep, send, links_v, sem):
    second = (pos[0] & 1) == 1
    rows = keep.shape[1]
    copy = pltpu.make_async_copy(links, links_v, sem)
    copy.start()
    copy.wait()
    a, b = links_v[:, :rows], links_v[:, rows:]
    keep[...] = jnp.where(second, b, a)
    send[...] = jnp.where(second, a, b)


def order_kernel(pos, vectors, pair, order, momenta, pairs, ordered, first, momenta_out, index, *scratch):
    vectors_v, ordering, pairs_v, sems = scratch
    nt, comps, count, sites = vectors.shape
    t = pos[0] & (nt - 1)
    up = pos[0] & 1
    copies = [
        pltpu.make_async_copy(vectors.at[t], vectors_v.at[up], sems.at[0]),
        pltpu.make_async_copy(pair.at[t], vectors_v.at[1 - up], sems.at[1]),
        pltpu.make_async_copy(order, ordering, sems.at[2]),
        pltpu.make_async_copy(momenta, momenta_out, sems.at[3]),
        pltpu.make_async_copy(pairs, pairs_v, sems.at[4]),
    ]
    for copy in copies:
        copy.start()
    row = lax.broadcasted_iota(jnp.int32, (count, count), 0)
    for copy in copies:
        copy.wait()
    low = jnp.minimum(pairs_v[0:1, :], pairs_v[1:2, :])
    high = jnp.maximum(pairs_v[0:1, :], pairs_v[1:2, :])
    index[...] = low * nt - (low * (low - 1)) // 2 + (high - low)
    hot = jnp.where(row == ordering[pl.ds(t, 1), :], 1.0, 0.0).T.astype(BF16)
    for p in range(2):
        for c in range(comps):
            picked = jnp.dot(hot, vectors_v[p, c], preferred_element_type=F32).astype(BF16)
            m, r = c // 2, c % 2
            rows, cols = slice(r * count, (r + 1) * count), slice(m * sites, (m + 1) * sites)
            ordered[p, rows, cols] = picked
            if p == 0:
                first[rows, cols] = picked


def move_kernel(total_x, pos, momenta, ordered, out_y, out_z, phase):
    planes, _, width = ordered.shape
    sites = width // 3
    src = lax.broadcasted_iota(jnp.int32, (sites, sites), 0)
    dst = lax.broadcasted_iota(jnp.int32, (sites, sites), 1)
    to_y = (dst + LZ) & (sites - 1)
    to_z = jnp.where((dst & (LZ - 1)) < LZ - 1, dst + 1, dst - (LZ - 1))
    for out, to in ((out_y, to_y), (out_z, to_z)):
        hot = jnp.where(src == to, 1.0, 0.0).astype(BF16)
        for p in range(planes):
            for a in range(3):
                at = slice(a * sites, (a + 1) * sites)
                out[p, :, at] = jnp.dot(
                    ordered[p, :, at], hot, preferred_element_type=F32
                ).astype(BF16)
    nops = momenta.shape[0]
    shape = (4 * nops, 128)
    row = lax.broadcasted_iota(jnp.int32, shape, 0)
    site = (row & 1) * 128 + lax.broadcasted_iota(jnp.int32, shape, 1)
    x_at = (pos[0] >> 1) * 2 + ((row >> 1) & 1)
    y_at, z_at = site // LZ, site & (LZ - 1)
    period = total_x * LY * LZ
    number = jnp.zeros(shape, jnp.int32)
    for k in range(nops):
        here = (
            momenta[k : k + 1, 0:1] * x_at * (LY * LZ)
            + momenta[k : k + 1, 1:2] * y_at * (total_x * LZ)
            + momenta[k : k + 1, 2:3] * z_at * (total_x * LY)
        )
        number = jnp.where((row >> 2) == k, here, number)
    number = number & (period - 1)
    quarter = period // 4
    turn = (number + quarter // 2) // quarter
    angle = (number - turn * quarter).astype(F32) * (2.0 * math.pi / period)
    sq = angle * angle
    sin = 1.0 / 362880.0
    for d in (-5040.0, 120.0, -6.0, 1.0):
        sin = sin * sq + 1.0 / d
    sin = sin * angle
    cos = -1.0 / 3628800.0
    for d in (40320.0, -720.0, 24.0, -2.0, 1.0):
        cos = cos * sq + 1.0 / d
    turn = turn & 3
    odd = (turn & 1) == 1
    big, small = jnp.where(odd, sin, cos), jnp.where(odd, cos, sin)
    phase[0] = jnp.where((turn == 1) | (turn == 2), -big, big)
    phase[1] = -jnp.where(turn >= 2, -small, small)


def elemental_kernel(scale, ops, pos, links, phase, ordered, *refs):
    nears, (send, keep, right) = refs[:-3], refs[-3:]
    planes, rows, width = ordered.shape
    count, sites = rows // 2, width // 3
    up = (pos[0] >> 1) & 1
    sub = 16
    grams = []
    for at, k in enumerate(ops):
        m = k % 3
        near = nears[at % len(nears)] if m else None
        gram = None
        for p in range(planes):
            for h in range(2):
                pr, pi = (phase[r, 4 * k + 2 * p + h : 4 * k + 2 * p + h + 1, :] for r in range(2))
                coef = []
                for e in range(9):
                    c = 18 * m + 2 * e
                    cr, ci = (links[c + r, 2 * p + h : 2 * p + h + 1, :] for r in range(2))
                    both = (pr * cr - pi * ci, pr * ci + pi * cr)
                    coef.append([jnp.broadcast_to(v, (sub, 128)) for v in both])
                for i in range(count // sub):
                    v = []
                    for b in range(3):
                        lo = b * sites + h * 128
                        cols = slice(lo, lo + 128)
                        parts = []
                        for r in range(2):
                            at_rows = slice(r * count + i * sub, r * count + (i + 1) * sub)
                            if m:
                                got = near[p, at_rows, cols]
                            elif p + 1 < planes:
                                got = ordered[p + 1, at_rows, cols]
                            else:
                                got = nears[0][at_rows, cols]
                            parts.append(got.astype(F32))
                        v.append(parts)
                    for a in range(3):
                        got = total([cmul(coef[3 * a + b], v[b]) for b in range(3)])
                        lo = a * sites + h * 128
                        for r in range(2):
                            at_rows = slice(r * count + i * sub, r * count + (i + 1) * sub)
                            right[at, p, at_rows, lo : lo + 128] = got[r].astype(BF16)
            part = lax.dot_general(
                ordered[p], right[at, p], (((1,), (1,)), ((), ())), preferred_element_type=F32
            )
            gram = part if gram is None else gram + part
        grams.append(
            (
                (gram[:count, :count] + gram[count:, count:]) * scale,
                (gram[:count, count:] - gram[count:, :count]) * scale,
            )
        )
    for r in range(2):
        first, second = grams[0][r], grams[1][r]
        send[r] = jnp.where(up == 1, first, second).astype(send.dtype)
        keep[r] = jnp.where(up == 1, second, first)


def split_kernel(pos, early, early_in, late, late_in, send, keep):
    up = ((pos[0] >> 2) & 1) == 1
    a = early[...] + early_in[...].astype(F32)
    b = late[...] + late_in[...].astype(F32)
    send[...] = jnp.where(up, a, b).astype(send.dtype)
    keep[...] = jnp.where(up, b, a)


def add_kernel(mine, other, out):
    out[...] = (mine[...].astype(F32) + other[...].astype(F32)).astype(out.dtype)


def trace_kernel(pos, mine, other, mine_b, other_b, tau, *outs):
    nt, count = tau.shape[0], tau.shape[-1]
    parity = pos[0] & (nt - 1)
    per, ib = mine_b.shape[1], mine_b.shape[2]
    for at, out in enumerate(outs):
        d = pos[0] ^ (2 * at)
        a, b = mine_b[:, d % per], other_b[:, d % per]
        picked = jnp.where((d // per) == parity, a, b)
        for r in range(2):
            out[r * ib : (r + 1) * ib, :] = picked[r]
    phi = []
    for t in range(nt):
        own, oth = mine[...], other[...]
        x = jnp.where(parity == t, own, oth).reshape(2 * count, count)
        hi = x.astype(BF16)
        lo = (x - hi.astype(F32)).astype(BF16)
        phi.append(jnp.concatenate([hi, lo], axis=0))
    prod = {}
    for t in range(nt):
        for u in range(nt):
            right = jnp.concatenate([tau[t, u, 0], tau[t, u, 1]], axis=1)
            got = jnp.dot(phi[t], right, preferred_element_type=F32)
            got = got[: 2 * count] + got[2 * count :]
            prod[t, u] = (
                got[:count, :count] - got[count:, count:],
                got[:count, count:] + got[count:, :count],
            )
    rows = []
    for t in range(nt):
        for u in range(t, nt):
            xr, xi = prod[t, u]
            yr, yi = prod[u, t][0].T, prod[u, t][1].T
            rows.append(jnp.sum(xr * yr - xi * yi, axis=0, keepdims=True))
            rows.append(jnp.sum(xr * yi + xi * yr, axis=0, keepdims=True))
    base = 2 * ib
    for out in outs:
        for at, v in enumerate(rows):
            out[base + at : base + at + 1, :] = v
        out[base + len(rows) :, :] = jnp.zeros_like(out[base + len(rows) :, :])


def final_kernel(ib, pos, chosen, *refs):
    parts, (out, corr) = [ref[...] for ref in refs[:4]], refs[4:]
    at = (pos[0] >> 1) & 3
    index = chosen[...]
    combos = (parts[0].shape[0] - 2 * ib) // 2
    for k in range(4):
        home = (2, 0, 1, 3)[k]
        v = parts[0]
        for flip in range(1, 4):
            v = jnp.where((at ^ flip) == home, parts[flip], v)
        for r in range(2):
            out[k, pl.ds(r, ib, stride=2), :] = v[r * ib : (r + 1) * ib]
        sums = jnp.sum(v[2 * ib :], axis=1, keepdims=True)
        for r in range(2):
            line = jnp.zeros(index.shape, F32)
            for j in range(combos):
                value = jnp.broadcast_to(sums[2 * j + r : 2 * j + r + 1, :], index.shape)
                line = jnp.where(index == j, value, line)
            corr[k, r : r + 1, :] = line


def on_device(vectors, gauge_links, perambulators, time_pairs, ordering, op_momenta):
    devices = lax.axis_size("space")
    pos = lax.axis_index("space").astype(jnp.int32).reshape(1)
    nt, count, comps, planes, sites = vectors.shape
    nops = op_momenta.shape[0]
    total_x = planes * devices
    assert planes == 1 and nt == 2 and nops == 4 and devices >= 8
    assert devices & (devices - 1) == 0 and sites == LY * LZ == 256
    scale = (3.0 * total_x * LY * LZ) ** (-0.5)

    natural = jnp.transpose(vectors, (0, 2, 3, 1, 4)).reshape(nt, comps, count, sites)
    own = gauge_links.reshape(54, nt * 2, 128)
    rows = 4
    wide = (2, 2 * count, 3 * sites)
    half = (54, rows // 2, 128)
    links_keep, links_send = call(
        split_links_kernel,
        [(half, F32), (half, F32)],
        [pos, own],
        scalars=1,
        loose=1,
        scratch=[pltpu.VMEM((54, rows, 128), F32), pltpu.SemaphoreType.DMA],
    )
    edge = ((54, 3 * rows // 2, 128), BF16)
    chip_links, edge_up, edge_down = call(
        pack_kernel,
        [((54, rows, 128), F32), edge, edge],
        [pos, links_keep, swapped(links_send, 1)],
        scalars=1,
    )
    below, above = shifted(edge_up, 2), shifted(edge_down, -2)
    npair = time_pairs.shape[0]
    ordered, first, momenta, chosen = call(
        order_kernel,
        [(wide, BF16), (wide[1:], BF16), (op_momenta.shape, jnp.int32), ((1, npair), jnp.int32)],
        [pos, natural, swapped(natural, 1), ordering, op_momenta, time_pairs.T],
        scalars=1,
        loose=5,
        scratch=[
            pltpu.VMEM((2, comps, count, sites), BF16),
            pltpu.VMEM((nt, count), jnp.int32),
            pltpu.VMEM((2, npair), jnp.int32),
            pltpu.SemaphoreType.DMA((5,)),
        ],
    )
    near_x = shifted(first, -2)
    near_y, near_z, phase = call(
        lambda *refs: move_kernel(total_x, *refs),
        [(wide, BF16), (wide, BF16), ((2, 4 * nops, 128), F32)],
        [pos, momenta, ordered],
        scalars=1,
    )
    (smeared,) = call(
        smear_kernel,
        [((54, rows, 128), F32)],
        [below, chip_links, above],
        scratch=[pltpu.VMEM((3, 54, 24, 128), F32), pltpu.VMEM((2, 18, 24, 128), F32)],
    )
    flat = (2, count, count)

    def grams(ops, nears, kind):
        return call(
            lambda *refs: elemental_kernel(scale, ops, *refs),
            [(flat, kind), (flat, F32)],
            [pos, smeared, phase, ordered] + nears,
            scalars=1,
            scratch=[pltpu.VMEM((2,) + wide, BF16)],
        )

    send, early = grams((1, 2), [near_y, near_z], F32)
    early_in = swapped(send, 2)
    send, late = grams((0, 3), [near_x], BF16)
    late_in = swapped(send, 2)
    send, keep = call(
        split_kernel, [(flat, F32), (flat, F32)], [pos, early, early_in, late, late_in], scalars=1
    )
    bit = 8
    other = swapped(send, 4)
    while bit <= devices:
        (keep,) = call(add_kernel, [(flat, BF16 if bit < devices else F32)], [keep, other])
        other = swapped(keep, bit if bit < devices else 1)
        bit *= 2
    mine = keep
    ib = nt * count // devices
    per = devices // nt
    blocks = call(
        trace_kernel,
        [((2 * ib + 8, 128), F32)] * 4,
        [
            pos,
            mine,
            other,
            mine.reshape(2, per, ib, count),
            other.reshape(2, per, ib, count),
            perambulators,
        ],
        scalars=1,
    )
    parts = [blocks[0]] + [swapped(blocks[f], 2 * f) for f in range(1, 4)]
    out, corr = call(
        lambda *refs: final_kernel(ib, *refs),
        [((nops, 2 * ib, count), F32), ((nops, 2, npair), F32)],
        [pos, chosen] + parts,
        scalars=1,
    )
    return out, jnp.transpose(corr, (0, 2, 1))


def solution(mesh):
    return jax.shard_map(
        on_device,
        mesh=mesh,
        in_specs=(
            P("grp", None, None, "space", None),
            P(None, None, "grp", "space", None),
            P("grp", None, None, None, None),
            P("grp", None),
            P("grp", None),
            P(),
        ),
        out_specs=(P("grp", "space", None), P("grp", None, None)),
        check_vma=False,
    )
```

```python
import math

import jax
import jax.numpy as jnp
from jax import lax
from jax.experimental import pallas as pl
from jax.experimental.pallas import tpu as pltpu
from jax.sharding import PartitionSpec as P


LY = 16
LZ = 16
RHO = 0.1


F32 = jnp.float32
BF16 = jnp.bfloat16


def vmem():
    return pl.BlockSpec(memory_space=pltpu.VMEM)


def smem():
    return pl.BlockSpec(memory_space=pltpu.SMEM)


def call(kernel, outs, ins, scalars=0, scratch=(), loose=0, flops=1000000, limit=16 << 20):
    run = pl.pallas_call(
        kernel,
        out_shape=[jax.ShapeDtypeStruct(s, d) for s, d in outs],
        in_specs=[smem()] * scalars
        + [vmem()] * (len(ins) - scalars - loose)
        + [pl.BlockSpec(memory_space=pltpu.HBM)] * loose,
        out_specs=[vmem()] * len(outs),
        scratch_shapes=list(scratch),
        compiler_params=pltpu.CompilerParams(vmem_limit_bytes=limit),
        cost_estimate=pl.CostEstimate(flops=flops, bytes_accessed=1000000, transcendentals=0),
    )
    first = len(ins) - loose
    ins = ins[:first] + [pltpu.with_memory_space_constraint(x, pltpu.HBM) for x in ins[first:]]
    return run(*ins)


def shifted(value, by):
    size = lax.axis_size("space")
    return lax.ppermute(value, "space", [(i, (i + by) % size) for i in range(size)])


def swapped(value, bit):
    size = lax.axis_size("space")
    return lax.ppermute(value, "space", [(i, i ^ bit) for i in range(size)])


def cmul(x, y):
    return (x[0] * y[0] - x[1] * y[1], x[0] * y[1] + x[1] * y[0])


def cadd(x, y):
    return (x[0] + y[0], x[1] + y[1])


def conj_mul(x, y):
    return (x[0] * y[0] + x[1] * y[1], x[0] * y[1] - x[1] * y[0])


def mul_conj(x, y):
    return (x[0] * y[0] + x[1] * y[1], x[1] * y[0] - x[0] * y[1])


def total(terms):
    out = terms[0]
    for t in terms[1:]:
        out = cadd(out, t)
    return out


R3 = range(3)


def mm(x, y):
    return [[total([cmul(x[a][c], y[c][b]) for c in R3]) for b in R3] for a in R3]


def mm_h(x, y):
    return [[total([mul_conj(x[a][c], y[b][c]) for c in R3]) for b in R3] for a in R3]


def h_mm(x, y):
    return [[total([conj_mul(x[c][a], y[c][b]) for c in R3]) for b in R3] for a in R3]


OFF = ((0, 1), (0, 2), (1, 2))


def anti(entry, imag):
    out = [imag(a, a) for a in R3]
    for a, b in OFF:
        up, low = entry(a, b), entry(b, a)
        out += [up[0] - low[0], up[1] + low[1]]
    return out


def anti_mm(x, y):
    def imag(a, b):
        terms = [x[a][c][0] * y[c][b][1] + x[a][c][1] * y[c][b][0] for c in R3]
        return terms[0] + terms[1] + terms[2]

    return anti(lambda a, b: total([cmul(x[a][c], y[c][b]) for c in R3]), imag)


def anti_mm_h(x, y):
    def imag(a, b):
        terms = [x[a][c][1] * y[b][c][0] - x[a][c][0] * y[b][c][1] for c in R3]
        return terms[0] + terms[1] + terms[2]

    return anti(lambda a, b: total([mul_conj(x[a][c], y[b][c]) for c in R3]), imag)


def exp_series(w):
    mean = (w[0] + w[1] + w[2]) * (RHO / 3.0)
    h = [w[a] * RHO - mean for a in R3]
    z = {}
    for at, (a, b) in enumerate(OFF):
        z[a, b] = (w[3 + 2 * at] * (0.5 * RHO), w[4 + 2 * at] * (0.5 * RHO))
    size = {ab: v[0] * v[0] + v[1] * v[1] for ab, v in z.items()}
    s_diag = [
        -(h[0] * h[0] + size[0, 1] + size[0, 2]),
        -(h[1] * h[1] + size[0, 1] + size[1, 2]),
        -(h[2] * h[2] + size[0, 2] + size[1, 2]),
    ]

    def turned(v, by):
        return (-by * v[1], by * v[0])

    neg = lambda v: (-v[0], -v[1])
    s = {
        (0, 1): cadd(turned(z[0, 1], h[0] + h[1]), neg(mul_conj(z[0, 2], z[1, 2]))),
        (0, 2): cadd(turned(z[0, 2], h[0] + h[2]), cmul(z[0, 1], z[1, 2])),
        (1, 2): cadd(turned(z[1, 2], h[1] + h[2]), neg(conj_mul(z[0, 1], z[0, 2]))),
    }
    p = 0.5 * (s_diag[0] + s_diag[1] + s_diag[2])
    ha, hb, hc = [(z[ab][1], -z[ab][0]) for ab in OFF]
    triple = cmul(ha, hc)
    det = (
        h[0] * (h[1] * h[2] - size[1, 2])
        - h[1] * size[0, 2]
        - h[2] * size[0, 1]
        + 2.0 * (triple[0] * hb[0] + triple[1] * hb[1])
    )
    k = -det
    f0 = (1.0 - (k * (1.0 / 720.0)) * k, k * (1.0 / 6.0 + p * (1.0 / 120.0)))
    f1 = (1.0 + p * (1.0 / 6.0) + (p * (1.0 / 120.0)) * p, k * (1.0 / 24.0 + p * (1.0 / 360.0)))
    f2 = (0.5 + p * (1.0 / 24.0) + (p * (1.0 / 720.0)) * p, k * (1.0 / 120.0))
    out = [[None] * 3 for _ in R3]
    for a in R3:
        out[a][a] = (
            f0[0] - f1[1] * h[a] + f2[0] * s_diag[a],
            f0[1] + f1[0] * h[a] + f2[1] * s_diag[a],
        )
    for a, b in OFF:
        (zr, zi), (sr, si) = z[a, b], s[a, b]
        rr, ri, ir, ii = f1[0] * zr, f1[0] * zi, f1[1] * zr, f1[1] * zi
        tr, ti, ur, ui = f2[0] * sr, f2[0] * si, f2[1] * sr, f2[1] * si
        out[a][b] = (rr - ii + tr - ui, ri + ir + ti + ur)
        out[b][a] = (tr + ui - rr - ii, ri - ir + ur - ti)
    return out


def pack_kernel(pos, links, links_in, chip, edge_up, edge_down):
    second = (pos[0] & 1) == 1
    half = links.shape[1]
    a, b = links[...], links_in[...]
    planes = (jnp.where(second, b, a), jnp.where(second, a, b))
    high = [v.astype(BF16) for v in planes]
    low = [(v - h.astype(F32)).astype(BF16) for v, h in zip(planes, high)]
    for at in range(2):
        chip[:, half * at : half * (at + 1), :] = planes[at]
    for out, parts in ((edge_up, high + [low[1]]), (edge_down, high + [low[0]])):
        for at, v in enumerate(parts):
            out[:, half * at : half * (at + 1), :] = v


def smear_kernel(below, own, above, out, links, moved):
    rows = own.shape[1] // 2
    low, high = below[...].astype(F32), above[...].astype(F32)
    parts = (
        low[:, :rows],
        low[:, rows : 2 * rows] + low[:, 2 * rows :],
        own[:, :rows],
        own[:, rows:],
        high[:, :rows] + high[:, 2 * rows :],
        high[:, rows : 2 * rows],
    )
    for at, part in enumerate(parts):
        links[0, :, rows * at : rows * (at + 1), :] = part
    tile = 4 * rows
    lane = lax.broadcasted_iota(jnp.int32, (tile, 128), 1)
    row = lax.broadcasted_iota(jnp.int32, (tile, 128), 0)
    even = (row & 1) == 0
    z_at = lane & (LZ - 1)

    def flip(x):
        return jnp.where(even, pltpu.roll(x, tile - 1, 0), pltpu.roll(x, 1, 0))

    def ahead_y(x):
        x = pltpu.roll(x, 128 - LZ, 1)
        return jnp.where(lane < 128 - LZ, x, flip(x))

    def behind_y(x):
        x = pltpu.roll(x, LZ, 1)
        return jnp.where(lane >= LZ, x, flip(x))

    def ahead_z(x):
        return jnp.where(z_at < LZ - 1, pltpu.roll(x, 127, 1), pltpu.roll(x, LZ - 1, 1))

    def behind_z(x):
        return jnp.where(z_at > 0, pltpu.roll(x, 1, 1), pltpu.roll(x, 128 - LZ + 1, 1))

    moved[...] = jnp.zeros_like(moved)

    def step(j, carry):
        source = jnp.where(j == 2, 1, 0)
        base = jnp.where(j == 2, rows, tile * j)
        target = jnp.where(j == 2, 2, 1)
        write = jnp.where(j == 2, 0, tile * j)
        base = pl.multiple_of(base, rows)
        write = pl.multiple_of(write, rows)

        def raw(c, off=0):
            return links[source, c, pl.ds(base + off, tile), :]

        def matrix(m, move=None, off=0):
            move = move or (lambda v: v)
            at = lambda a, b, r: move(raw(18 * m + 2 * (3 * a + b) + r, off))
            return [[(at(a, b, 0), at(a, b, 1)) for b in R3] for a in R3]

        def ahead(m, n):
            if n == 0:
                return matrix(m, None, rows)
            return matrix(m, ahead_y if n == 1 else ahead_z)

        def behind(values, n, slot):
            if n == 1:
                return [behind_y(v) for v in values]
            if n == 2:
                return [behind_z(v) for v in values]
            back = []
            for c, v in enumerate(values):
                moved[source, 9 * slot + c, pl.ds(base + rows, tile), :] = v
                back.append(moved[source, 9 * slot + c, pl.ds(base, tile), :])
            return back

        w = [None, None, None]

        def give(m, values, sign):
            if w[m] is None:
                assert sign > 0
                w[m] = values
            else:
                w[m] = [a + b if sign > 0 else a - b for a, b in zip(w[m], values)]

        for m, n in ((0, 1), (2, 0), (1, 2)):
            um, un = matrix(m), matrix(n)
            y = mm_h(ahead(n, m), ahead(m, n))
            x = h_mm(un, um)
            plaq = anti_mm_h(mm_h(un, y), um)
            give(m, plaq, 1)
            q_m = anti_mm(x, y)
            q_n = anti_mm(y, x)
            slot = 0 if 1 in (m, n) else 1
            give(m, behind(q_m, n, slot), 1)
            if w[n] is None:
                w[n] = [-a for a in plaq]
            else:
                give(n, plaq, -1)
            give(n, behind(q_n, m, slot), -1)
        for m in R3:
            new = mm(exp_series(w[m]), matrix(m))
            for a in R3:
                for b in R3:
                    for r in range(2):
                        c = 18 * m + 2 * (3 * a + b) + r
                        links[target, c, pl.ds(write, tile), :] = new[a][b][r]
        return carry

    lax.fori_loop(0, 3, step, 0)
    out[...] = links[2, :, rows : 3 * rows, :]


def split_links_kernel(pos, links, keep, send, links_v, sem):
    second = (pos[0] & 1) == 1
    rows = keep.shape[1]
    copy = pltpu.make_async_copy(links, links_v, sem)
    copy.start()
    copy.wait()
    a, b = links_v[:, :rows], links_v[:, rows:]
    keep[...] = jnp.where(second, b, a)
    send[...] = jnp.where(second, a, b)


def order_kernel(pos, vectors, pair, order, momenta, pairs, ordered, first, momenta_out, index, *scratch):
    vectors_v, ordering, pairs_v, sems = scratch
    nt, comps, count, sites = vectors.shape
    t = pos[0] & (nt - 1)
    up = pos[0] & 1
    copies = [
        pltpu.make_async_copy(vectors.at[t], vectors_v.at[up], sems.at[0]),
        pltpu.make_async_copy(pair.at[t], vectors_v.at[1 - up], sems.at[1]),
        pltpu.make_async_copy(order, ordering, sems.at[2]),
        pltpu.make_async_copy(momenta, momenta_out, sems.at[3]),
        pltpu.make_async_copy(pairs, pairs_v, sems.at[4]),
    ]
    for copy in copies:
        copy.start()
    row = lax.broadcasted_iota(jnp.int32, (count, count), 0)
    for copy in copies:
        copy.wait()
    low = jnp.minimum(pairs_v[0:1, :], pairs_v[1:2, :])
    high = jnp.maximum(pairs_v[0:1, :], pairs_v[1:2, :])
    index[...] = low * nt - (low * (low - 1)) // 2 + (high - low)
    hot = jnp.where(row == ordering[pl.ds(t, 1), :], 1.0, 0.0).T.astype(BF16)
    for p in range(2):
        for c in range(comps):
            picked = jnp.dot(hot, vectors_v[p, c], preferred_element_type=F32).astype(BF16)
            m, r = c // 2, c % 2
            rows, cols = slice(r * count, (r + 1) * count), slice(m * sites, (m + 1) * sites)
            ordered[p, rows, cols] = picked
            if p == 0:
                first[rows, cols] = picked


def move_kernel(total_x, pos, momenta, ordered, out_y, out_z, phase):
    planes, _, width = ordered.shape
    sites = width // 3
    src = lax.broadcasted_iota(jnp.int32, (sites, sites), 0)
    dst = lax.broadcasted_iota(jnp.int32, (sites, sites), 1)
    to_y = (dst + LZ) & (sites - 1)
    to_z = jnp.where((dst & (LZ - 1)) < LZ - 1, dst + 1, dst - (LZ - 1))
    for out, to in ((out_y, to_y), (out_z, to_z)):
        hot = jnp.where(src == to, 1.0, 0.0).astype(BF16)
        for p in range(planes):
            for a in range(3):
                at = slice(a * sites, (a + 1) * sites)
                out[p, :, at] = jnp.dot(
                    ordered[p, :, at], hot, preferred_element_type=F32
                ).astype(BF16)
    nops = momenta.shape[0]
    shape = (4 * nops, 128)
    row = lax.broadcasted_iota(jnp.int32, shape, 0)
    site = (row & 1) * 128 + lax.broadcasted_iota(jnp.int32, shape, 1)
    x_at = (pos[0] >> 1) * 2 + ((row >> 1) & 1)
    y_at, z_at = site // LZ, site & (LZ - 1)
    period = total_x * LY * LZ
    number = jnp.zeros(shape, jnp.int32)
    for k in range(nops):
        here = (
            momenta[k : k + 1, 0:1] * x_at * (LY * LZ)
            + momenta[k : k + 1, 1:2] * y_at * (total_x * LZ)
            + momenta[k : k + 1, 2:3] * z_at * (total_x * LY)
        )
        number = jnp.where((row >> 2) == k, here, number)
    number = number & (period - 1)
    quarter = period // 4
    turn = (number + quarter // 2) // quarter
    angle = (number - turn * quarter).astype(F32) * (2.0 * math.pi / period)
    sq = angle * angle
    sin = 1.0 / 362880.0
    for d in (-5040.0, 120.0, -6.0, 1.0):
        sin = sin * sq + 1.0 / d
    sin = sin * angle
    cos = -1.0 / 3628800.0
    for d in (40320.0, -720.0, 24.0, -2.0, 1.0):
        cos = cos * sq + 1.0 / d
    turn = turn & 3
    odd = (turn & 1) == 1
    big, small = jnp.where(odd, sin, cos), jnp.where(odd, cos, sin)
    phase[0] = jnp.where((turn == 1) | (turn == 2), -big, big)
    phase[1] = -jnp.where(turn >= 2, -small, small)


def elemental_kernel(scale, ops, planes, stage, pos, links, phase, ordered, *refs):
    count_outs = 2 if stage == "part" else 3
    nears, outs = refs[:-count_outs], refs[-count_outs:]
    right = outs[-1]
    if stage == "rest":
        before, nears = nears[0], nears[1:]
    rows, width = ordered.shape[1:]
    count, sites = rows // 2, width // 3
    up = (pos[0] >> 1) & 1
    sub = 16
    grams = []
    for at, k in enumerate(ops):
        m = k % 3
        near = nears[at] if m else None
        gram = before[at] if stage == "rest" else None
        for p in planes:
            for h in range(2):
                pr, pi = (phase[r, 4 * k + 2 * p + h : 4 * k + 2 * p + h + 1, :] for r in range(2))
                coef = []
                for e in range(9):
                    c = 18 * m + 2 * e
                    cr, ci = (links[c + r, 2 * p + h : 2 * p + h + 1, :] for r in range(2))
                    both = (pr * cr - pi * ci, pr * ci + pi * cr)
                    coef.append([jnp.broadcast_to(v, (sub, 128)) for v in both])
                for i in range(count // sub):
                    v = []
                    for b in range(3):
                        lo = b * sites + h * 128
                        cols = slice(lo, lo + 128)
                        parts = []
                        for r in range(2):
                            at_rows = slice(r * count + i * sub, r * count + (i + 1) * sub)
                            if m:
                                got = near[p, at_rows, cols]
                            elif p == 0:
                                got = ordered[p + 1, at_rows, cols]
                            else:
                                got = nears[0][at_rows, cols]
                            parts.append(got.astype(F32))
                        v.append(parts)
                    for a in range(3):
                        got = total([cmul(coef[3 * a + b], v[b]) for b in range(3)])
                        lo = a * sites + h * 128
                        for r in range(2):
                            at_rows = slice(r * count + i * sub, r * count + (i + 1) * sub)
                            right[at, p, at_rows, lo : lo + 128] = got[r].astype(BF16)
            part = lax.dot_general(
                ordered[p], right[at, p], (((1,), (1,)), ((), ())), preferred_element_type=F32
            )
            gram = part if gram is None else gram + part
        if stage == "part":
            outs[0][at] = gram
            continue
        grams.append(
            (
                (gram[:count, :count] + gram[count:, count:]) * scale,
                (gram[:count, count:] - gram[count:, :count]) * scale,
            )
        )
    if stage == "part":
        return
    send, keep = outs[:2]
    for r in range(2):
        first, second = grams[0][r], grams[1][r]
        send[r] = jnp.where(up == 1, first, second).astype(send.dtype)
        keep[r] = jnp.where(up == 1, second, first)


def split_kernel(pos, early, early_in, late, late_in, send, keep):
    up = ((pos[0] >> 2) & 1) == 1
    a = early[...] + early_in[...].astype(F32)
    b = late[...] + late_in[...].astype(F32)
    send[...] = jnp.where(up, a, b).astype(send.dtype)
    keep[...] = jnp.where(up, b, a)


def add_kernel(mine, other, out):
    out[...] = (mine[...].astype(F32) + other[...].astype(F32)).astype(out.dtype)


def trace_kernel(pos, mine, other, mine_b, other_b, tau, *outs):
    nt, count = tau.shape[0], tau.shape[-1]
    parity = pos[0] & (nt - 1)
    per, ib = mine_b.shape[1], mine_b.shape[2]
    for at, out in enumerate(outs):
        d = pos[0] ^ (2 * at)
        a, b = mine_b[:, d % per], other_b[:, d % per]
        picked = jnp.where((d // per) == parity, a, b)
        for r in range(2):
            out[r * ib : (r + 1) * ib, :] = picked[r]
    phi = []
    for t in range(nt):
        own, oth = mine[...], other[...]
        x = jnp.where(parity == t, own, oth).reshape(2 * count, count)
        hi = x.astype(BF16)
        lo = (x - hi.astype(F32)).astype(BF16)
        phi.append(jnp.concatenate([hi, lo], axis=0))
    prod = {}
    for t in range(nt):
        for u in range(nt):
            right = jnp.concatenate([tau[t, u, 0], tau[t, u, 1]], axis=1)
            got = jnp.dot(phi[t], right, preferred_element_type=F32)
            got = got[: 2 * count] + got[2 * count :]
            prod[t, u] = (
                got[:count, :count] - got[count:, count:],
                got[:count, count:] + got[count:, :count],
            )
    rows = []
    for t in range(nt):
        for u in range(t, nt):
            xr, xi = prod[t, u]
            yr, yi = prod[u, t][0].T, prod[u, t][1].T
            rows.append(jnp.sum(xr * yr - xi * yi, axis=0, keepdims=True))
            rows.append(jnp.sum(xr * yi + xi * yr, axis=0, keepdims=True))
    base = 2 * ib
    for out in outs:
        for at, v in enumerate(rows):
            out[base + at : base + at + 1, :] = v
        out[base + len(rows) :, :] = jnp.zeros_like(out[base + len(rows) :, :])


def final_kernel(ib, pos, chosen, *refs):
    parts, (out, corr) = [ref[...] for ref in refs[:4]], refs[4:]
    at = (pos[0] >> 1) & 3
    index = chosen[...]
    combos = (parts[0].shape[0] - 2 * ib) // 2
    for k in range(4):
        home = (2, 0, 1, 3)[k]
        v = parts[0]
        for flip in range(1, 4):
            v = jnp.where((at ^ flip) == home, parts[flip], v)
        for r in range(2):
            out[k, pl.ds(r, ib, stride=2), :] = v[r * ib : (r + 1) * ib]
        sums = jnp.sum(v[2 * ib :], axis=1, keepdims=True)
        for r in range(2):
            line = jnp.zeros(index.shape, F32)
            for j in range(combos):
                value = jnp.broadcast_to(sums[2 * j + r : 2 * j + r + 1, :], index.shape)
                line = jnp.where(index == j, value, line)
            corr[k, r : r + 1, :] = line


def on_device(vectors, gauge_links, perambulators, time_pairs, ordering, op_momenta):
    devices = lax.axis_size("space")
    pos = lax.axis_index("space").astype(jnp.int32).reshape(1)
    nt, count, comps, planes, sites = vectors.shape
    nops = op_momenta.shape[0]
    total_x = planes * devices
    assert planes == 1 and nt == 2 and nops == 4 and devices >= 8
    assert devices & (devices - 1) == 0 and sites == LY * LZ == 256
    scale = (3.0 * total_x * LY * LZ) ** (-0.5)

    natural = jnp.transpose(vectors, (0, 2, 3, 1, 4)).reshape(nt, comps, count, sites)
    own = gauge_links.reshape(54, nt * 2, 128)
    rows = 4
    wide = (2, 2 * count, 3 * sites)
    half = (54, rows // 2, 128)
    links_keep, links_send = call(
        split_links_kernel,
        [(half, F32), (half, F32)],
        [pos, own],
        scalars=1,
        loose=1,
        scratch=[pltpu.VMEM((54, rows, 128), F32), pltpu.SemaphoreType.DMA],
    )
    edge = ((54, 3 * rows // 2, 128), BF16)
    chip_links, edge_up, edge_down = call(
        pack_kernel,
        [((54, rows, 128), F32), edge, edge],
        [pos, links_keep, swapped(links_send, 1)],
        scalars=1,
    )
    below, above = shifted(edge_up, 2), shifted(edge_down, -2)
    npair = time_pairs.shape[0]
    ordered, first, momenta, chosen = call(
        order_kernel,
        [(wide, BF16), (wide[1:], BF16), (op_momenta.shape, jnp.int32), ((1, npair), jnp.int32)],
        [pos, natural, swapped(natural, 1), ordering, op_momenta, time_pairs.T],
        scalars=1,
        loose=5,
        scratch=[
            pltpu.VMEM((2, comps, count, sites), BF16),
            pltpu.VMEM((nt, count), jnp.int32),
            pltpu.VMEM((2, npair), jnp.int32),
            pltpu.SemaphoreType.DMA((5,)),
        ],
    )
    near_x = shifted(first, -2)
    near_y, near_z, phase = call(
        lambda *refs: move_kernel(total_x, *refs),
        [(wide, BF16), (wide, BF16), ((2, 4 * nops, 128), F32)],
        [pos, momenta, ordered],
        scalars=1,
    )
    (smeared,) = call(
        smear_kernel,
        [((54, rows, 128), F32)],
        [below, chip_links, above],
        scratch=[pltpu.VMEM((3, 54, 24, 128), F32), pltpu.VMEM((2, 18, 24, 128), F32)],
    )
    flat = (2, count, count)

    def grams(ops, planes, stage, nears, outs):
        return call(
            lambda *refs: elemental_kernel(scale, ops, planes, stage, *refs),
            outs,
            [pos, smeared, phase, ordered] + nears,
            scalars=1,
            scratch=[pltpu.VMEM((2,) + wide, BF16)],
        )

    send, early = grams((1, 2), (0, 1), "all", [near_y, near_z], [(flat, F32), (flat, F32)])
    early_in = swapped(send, 2)
    (part,) = grams((0, 3), (0,), "part", [], [((2, 2 * count, 2 * count), F32)])
    send, late = grams((0, 3), (1,), "rest", [part, near_x], [(flat, BF16), (flat, F32)])
    late_in = swapped(send, 2)
    send, keep = call(
        split_kernel, [(flat, BF16), (flat, F32)], [pos, early, early_in, late, late_in], scalars=1
    )
    bit = 8
    other = swapped(send, 4)
    while bit <= devices:
        (keep,) = call(add_kernel, [(flat, BF16 if bit < devices else F32)], [keep, other])
        other = swapped(keep, bit if bit < devices else 1)
        bit *= 2
    mine = keep
    ib = nt * count // devices
    per = devices // nt
    blocks = call(
        trace_kernel,
        [((2 * ib + 8, 128), F32)] * 4,
        [
            pos,
            mine,
            other,
            mine.reshape(2, per, ib, count),
            other.reshape(2, per, ib, count),
            perambulators,
        ],
        scalars=1,
    )
    parts = [blocks[0]] + [swapped(blocks[f], 2 * f) for f in range(1, 4)]
    out, corr = call(
        lambda *refs: final_kernel(ib, *refs),
        [((nops, 2 * ib, count), F32), ((nops, 2, npair), F32)],
        [pos, chosen] + parts,
        scalars=1,
    )
    return out, jnp.transpose(corr, (0, 2, 1))


def solution(mesh):
    return jax.shard_map(
        on_device,
        mesh=mesh,
        in_specs=(
            P("grp", None, None, "space", None),
            P(None, None, "grp", "space", None),
            P("grp", None, None, None, None),
            P("grp", None),
            P("grp", None),
            P(),
        ),
        out_specs=(P("grp", "space", None), P("grp", None, None)),
        check_vma=False,
    )
```
